32 devices in a mesh: groups: 2 (over y), expert: 4 (over z), dp: 2 (over x), pair: 2 (over core).
Axes of the slice: x: 2, y: 2, z: 4, core: 2. Of those that a mesh axis runs over, the one named last changes fastest.
Arguments:
- tokens: bfloat16 [4096, 2048], P(('groups', 'expert', 'dp', 'pair')), parts along dimension 0, may hold values from -6 to 6
- expert_ids: int32 [4096, 2], P(('groups', 'expert', 'dp', 'pair')), parts along dimension 0, may hold values from 0 to 7, all different within a row; in each aligned block of 128 rows (0 to 127, 128 to 255, ...) at most 36 rows name the same one
- gate_weights: float32 [4096, 2], P(('groups', 'expert', 'dp', 'pair')), parts along dimension 0, may hold values from 0.1 to 1
- upstream: bfloat16 [4096, 2048], P(('groups', 'expert', 'dp', 'pair')), parts along dimension 0, may hold values from -6 to 6
- w_gate: bfloat16 [8, 2048, 1408], P(('expert', 'pair'), 'dp'), may hold values from -0.125 to 0.125
- w_up: bfloat16 [8, 2048, 1408], P(('expert', 'pair'), 'dp'), may hold values from -0.125 to 0.125
- w_down: bfloat16 [8, 1408, 2048], P(('expert', 'pair'), 'dp'), may hold values from -0.15625 to 0.15625
Outputs:
- out: bfloat16 [4096, 2048], P(('groups', 'expert', 'dp', 'pair')), parts along dimension 0
- d_tokens: bfloat16 [4096, 2048], P(('groups', 'expert', 'dp', 'pair')), parts along dimension 0
- d_gates: float32 [4096, 2], P(('groups', 'expert', 'dp', 'pair')), parts along dimension 0
- grad_gate: bfloat16 [16, 2048, 1408], P(('groups', 'expert', 'pair'), 'dp'), parts along dimension 0
- grad_up: bfloat16 [16, 2048, 1408], P(('groups', 'expert', 'pair'), 'dp'), parts along dimension 0
- grad_down: bfloat16 [16, 1408, 2048], P(('groups', 'expert', 'pair'), 'dp'), parts along dimension 0
The draws below stay inside these ranges and needn't reach their ends.
There are 2 independent parts, one for each index of `groups`. The reference program is written for one: setup_inputs(seed, part) draws one part's arguments, and reference() takes and returns one part's arrays. A program takes and returns all parts, laid end to end along the dimension named above; an argument that names none is the same for every part. Nothing has to cross between parts.
Inputs may be any that keep to these rules, and one draw needn't show every extreme that they name: `expert_ids`: each token names 2 different experts; the 128 tokens of one device name one expert at most 36 times, and exactly 36 times in some blocks.
All inputs are finite; a program needn't handle non-finite values.
Results may differ from the reference program's by a relative error of at most 0.009.
Values may be sent and summed in bfloat16 or wider, within the bound.
No kernel may reach another device: no remote copies, remote signals or barrier semaphores. Data moves between devices by JAX's collectives and lax.ppermute only.
A program may use at most 128 MiB of HBM per device.

```python
import math
import jax
import jax.numpy as jnp
import numpy as np
from jax import lax

D = 2048
FF = 1408
TOP = 2
TOK_DEV = 128
EXPERTS = 8
CAP = 36
TOKENS = 2048
N_EXPERT = 4
N_DP = 2
N_PAIR = 2


def shard_levels(key, shape, split, least, high):
    gain = 1.0
    for dim, shards_of in split:
        heights = jax.random.uniform(jax.random.fold_in(jax.random.fold_in(key, 6), dim), (shards_of,), jnp.float32, least / len(split), high / len(split))
        gain = gain * jnp.repeat(jnp.exp(heights), shape[dim] // shards_of).reshape((-1,) + (1,) * (len(shape) - 1 - dim))
    return gain


def shared_out(stream_key, own, number, rows, number_of, top, limit, lean):
    sequence = jax.random.permutation(stream_key, number_of)
    heavy_load, common = shares(number_of, rows * top, limit, lean, True), shares(number_of, rows * top, limit, lean, False)
    places = jnp.arange(number_of)

    def named(sizes, rotation):
        used = int((sizes > 0).sum())
        fixed = max(1, used // 4)
        shifted = fixed + (places - fixed + rotation * (used - fixed)) % max(1, number_of - fixed)
        return jnp.zeros((number_of,), jnp.int32).at[sequence[jnp.where(places < fixed, places, shifted)]].set(jnp.asarray(sizes, jnp.int32))

    sizes = jnp.where(number % 4 == 0, named(heavy_load, number // 4), named(common, number - number // 4 - 1))
    mixed = jax.random.permutation(jax.random.fold_in(own, 3), number_of)
    donor, sink = mixed[0:number_of // 2 * 2:2], mixed[1:number_of // 2 * 2:2]
    room = jnp.minimum(sizes[donor] - 1, limit - sizes[sink]) // 2
    room = jnp.where((donor == sequence[0]) | (sink == sequence[0]) | (sizes[sink] == 0), 0, jnp.maximum(room, 0))
    shifted = jax.random.randint(jax.random.fold_in(own, 4), (number_of // 2,), 0, 1 << 20) % (room + 1)
    sizes = sizes.at[donor].add(-shifted).at[sink].add(shifted)
    items = jnp.searchsorted(jnp.cumsum(sizes), jnp.arange(rows * top), side="right").astype(jnp.int32)
    listing = items.reshape(top, rows).T
    listing = listing[jax.random.permutation(jax.random.fold_in(own, 1), rows)]
    rotation = jax.random.randint(jax.random.fold_in(own, 2), (rows, 1), 0, top)
    return jnp.take_along_axis(listing, (jnp.arange(top)[None, :] + rotation) % top, axis=1)


def shares(amount, total, limit, lean, full):
    weights = [(1 << 20) // math.isqrt(grade ** lean) + 1 for grade in range(1, amount + 1)]
    largest = limit if full else min(limit, max(-(-total // amount), total * weights[0] // sum(weights)))
    least = 1 if total - largest >= amount - 1 else 0
    given, surplus = [largest] + [least] * (amount - 1), total - largest - least * (amount - 1)
    while surplus > 0:
        free = [i for i in range(1, amount) if given[i] < largest] or [i for i in range(1, amount) if given[i] < limit]
        mass, left = sum([weights[i] for i in free]), surplus
        for i in free:
            more = min(limit - given[i], max(1, left * weights[i] // mass), surplus)
            given[i] = given[i] + more
            surplus = surplus - more
    return np.array(given)


def noise(key, extent, width, most, shards=(), held_as=jnp.bfloat16):
    values = width * jax.random.normal(key, extent, jnp.float32)
    if shards:
        values = values * shard_levels(key, extent, shards, -0.22, 0.18)
    return jnp.clip(values, -most, most).astype(held_as)


def setup_inputs(seed: int = 0, part: int = 0) -> dict:
    key_list = jax.random.split(jax.random.key(seed), 8)
    part_keys = jax.random.split(jax.random.fold_in(key_list[7], part), 8)
    tokens = noise(part_keys[0], (TOKENS, D), 1.0, 6.0, ((0, 16),))
    expert_ids_keys = jax.random.split(jax.random.fold_in(part_keys[1], 1), TOKENS // TOK_DEV)
    expert_ids_turns = jax.random.permutation(jax.random.fold_in(part_keys[1], 3), TOKENS // TOK_DEV)
    expert_ids = jax.vmap(lambda own, number: shared_out(jax.random.fold_in(part_keys[1], 2), own, number, TOK_DEV, EXPERTS, TOP, CAP, 2))(expert_ids_keys, expert_ids_turns).reshape((TOKENS, TOP))
    gate_weights = jnp.clip(jnp.exp(math.log(1.0) - 2.3025851 * jax.random.uniform(part_keys[2], (TOKENS, TOP), jnp.float32) ** shard_levels(part_keys[2], (TOKENS, TOP), ((0, 16),), -0.2, 0.2)), 0.1, 1.0)
    upstream = noise(part_keys[3], (TOKENS, D), 1.0, 6.0, ((0, 16),))
    w_gate = noise(key_list[4], (EXPERTS, D, FF), D ** -0.5, 0.125, ((0, 8), (1, 2)))
    w_up = noise(key_list[5], (EXPERTS, D, FF), D ** -0.5, 0.125, ((0, 8), (1, 2)))
    w_down = noise(key_list[6], (EXPERTS, FF, D), FF ** -0.5, 0.15625, ((0, 8), (1, 2)))
    return dict(tokens=tokens, expert_ids=expert_ids, gate_weights=gate_weights, upstream=upstream, w_gate=w_gate, w_up=w_up, w_down=w_down)


def expert_pass(inputs, scaled, gate_w, up_w, down_w):
    gate_pre = jnp.dot(inputs, gate_w, preferred_element_type=jnp.float32)
    up_pre = jnp.dot(inputs, up_w, preferred_element_type=jnp.float32)
    squash = jax.nn.sigmoid(gate_pre)
    active = gate_pre * squash
    hidden = (active * up_pre).astype(jnp.bfloat16)
    output = jnp.dot(hidden, down_w, preferred_element_type=jnp.float32).astype(jnp.bfloat16)
    hidden_grad = jnp.dot(scaled, down_w.T, preferred_element_type=jnp.float32)
    gate_grad = (hidden_grad * up_pre * (squash + active * (1.0 - squash))).astype(jnp.bfloat16)
    up_grad = (hidden_grad * active).astype(jnp.bfloat16)
    input_grad = (jnp.dot(gate_grad, gate_w.T, preferred_element_type=jnp.float32)
                  + jnp.dot(up_grad, up_w.T, preferred_element_type=jnp.float32)).astype(jnp.bfloat16)
    return hidden, output, gate_grad, up_grad, input_grad


def by_replica(values):
    return values.reshape(N_EXPERT, N_DP, N_PAIR * CAP, values.shape[1]).astype(jnp.float32)


def replica_sum(first_op, second_op):
    products = jnp.einsum("adrk,adrf->dkf", by_replica(first_op), by_replica(second_op))
    rounded = lax.optimization_barrier(products.astype(jnp.bfloat16))
    return jnp.sum(rounded.astype(jnp.float32), 0).astype(jnp.bfloat16)


def reference(tokens, expert_ids, gate_weights, upstream, w_gate, w_up, w_down):
    device_count = TOKENS // TOK_DEV
    per_device = TOK_DEV * TOP
    all_rows = TOKENS * TOP
    device_ids = expert_ids.reshape(device_count, per_device)
    onehot = (device_ids[:, :, None] == jnp.arange(EXPERTS, dtype=jnp.int32)[None, None, :]).astype(jnp.int32)
    position = jnp.sum(jnp.cumsum(onehot, 1) * onehot, 2) - 1
    device_rows = jnp.arange(device_count, dtype=jnp.int32)[:, None]
    columns = (device_rows * CAP + position).astype(jnp.int32)
    row_index = jnp.arange(all_rows, dtype=jnp.int32).reshape(device_count, per_device)
    slot_table = jnp.full((EXPERTS, device_count * CAP), all_rows, jnp.int32).at[device_ids, columns].set(row_index)
    zero_row = jnp.zeros((1, D), jnp.bfloat16)
    token_ext = jnp.concatenate([tokens, zero_row], 0)
    scaled = (gate_weights[:, :, None] * upstream.astype(jnp.float32)[:, None, :]).astype(jnp.bfloat16)
    scaled_ext = jnp.concatenate([scaled.reshape(all_rows, D), zero_row], 0)

    def one_expert(expert_id):
        slot_rows = slot_table[expert_id]
        rows_in = token_ext[slot_rows // TOP]
        grads_in = scaled_ext[slot_rows]
        hidden, output, gate_grad, up_grad, input_grad = expert_pass(
            rows_in, grads_in, w_gate[expert_id], w_up[expert_id], w_down[expert_id])
        grad_g = replica_sum(rows_in, gate_grad)
        grad_u = replica_sum(rows_in, up_grad)
        grad_d = replica_sum(hidden, grads_in)
        return output, input_grad, grad_g, grad_u, grad_d

    outputs, input_grads, grad_gate, grad_up, grad_down = lax.map(one_expert, jnp.arange(EXPERTS, dtype=jnp.int32))
    flat_slots = slot_table.reshape(-1)
    out_rows = jnp.zeros((all_rows + 1, D), jnp.bfloat16).at[flat_slots].set(outputs.reshape(-1, D))[:all_rows]
    grad_rows = jnp.zeros((all_rows + 1, D), jnp.bfloat16).at[flat_slots].set(input_grads.reshape(-1, D))[:all_rows]
    out_rows = out_rows.reshape(TOKENS, TOP, D).astype(jnp.float32)
    grad_rows = grad_rows.reshape(TOKENS, TOP, D).astype(jnp.float32)
    out = jnp.sum(gate_weights[:, :, None] * out_rows, 1).astype(jnp.bfloat16)
    d_gates = jnp.sum(upstream.astype(jnp.float32)[:, None, :] * out_rows, 2)
    d_tokens = jnp.sum(grad_rows, 1).astype(jnp.bfloat16)
    return (out, d_tokens, d_gates, grad_gate, grad_up, grad_down)
```

```python
import functools

import jax
import jax.numpy as jnp
from jax import lax
from jax.experimental import pallas as pl
from jax.experimental.pallas import tpu as pltpu
from jax.sharding import PartitionSpec as P


F32 = jnp.float32
BF16 = jnp.bfloat16
ANY = pl.BlockSpec(memory_space=pl.ANY)
VMEM = pl.BlockSpec(memory_space=pltpu.VMEM)
SMEM = pl.BlockSpec(memory_space=pltpu.SMEM)


def round_up(value, unit):
    return -(-value // unit) * unit


def cost(flops, moved):
    return pl.CostEstimate(flops=flops, bytes_accessed=moved, transcendentals=0)


def nbytes(*arrays):
    return sum(a.size * a.dtype.itemsize for a in arrays)


def select_rows(ids, experts, stride):
    chosen, rows = ids.shape
    lanes = lax.broadcasted_iota(jnp.int32, (experts, rows), 0)
    member = [(lanes == ids[k : k + 1, :]) for k in range(chosen)]
    count = sum(m.astype(F32) for m in member)
    before = lax.broadcasted_iota(jnp.int32, (rows, rows), 0) < lax.broadcasted_iota(jnp.int32, (rows, rows), 1)
    earlier = jnp.dot(count.astype(BF16), before.astype(F32).astype(BF16), preferred_element_type=F32)
    slots = lax.broadcasted_iota(jnp.int32, (experts * stride, rows), 0)
    picks = []
    for k in range(chosen):
        place = jnp.sum(jnp.where(member[k], earlier, 0.0), 0, keepdims=True).astype(jnp.int32)
        picks.append(slots == ids[k : k + 1, :] * stride + place)
    return picks


def dispatch_kernel(experts, capacity, ids_ref, gates_ref, tok_ref, ups_ref, rows_ref, grads_ref):
    stride = round_up(capacity, 8)
    picks = select_rows(ids_ref[...], experts, stride)
    scale = sum(
        jnp.sum(jnp.where(pick, gates_ref[k : k + 1, :], 0.0), 1, keepdims=True)
        for k, pick in enumerate(picks)
    )
    pick = sum(p.astype(F32) for p in picks).astype(BF16)
    width = tok_ref.shape[1]
    tile = 256

    @pl.loop(0, width // tile)
    def _(step):
        cols = pl.ds(pl.multiple_of(step * tile, tile), tile)
        rows = jnp.dot(pick, tok_ref[:, cols], preferred_element_type=F32)
        grads = jnp.dot(pick, ups_ref[:, cols], preferred_element_type=F32) * scale
        for e in range(experts):
            rows_ref[e, :, cols] = rows[e * stride : e * stride + capacity].astype(BF16)
            grads_ref[e, :, cols] = grads[e * stride : e * stride + capacity].astype(BF16)


def dispatch(ids, gates, tokens, upstream, experts, capacity):
    shape = jax.ShapeDtypeStruct((experts, capacity, tokens.shape[1]), BF16)
    return pl.pallas_call(
        functools.partial(dispatch_kernel, experts, capacity),
        out_shape=(shape, shape),
        in_specs=[VMEM] * 4,
        out_specs=(VMEM, VMEM),
        cost_estimate=cost(0, 2 * nbytes(tokens, upstream) * 3),
        name="dispatch",
    )(ids, gates, tokens, upstream)


def combine_out_kernel(experts, capacity, ids_ref, gates_ref, ups_ref, back_ref, out_ref, dgates_ref, full):
    stride = round_up(capacity, 8)
    fill_slots(experts, capacity, stride, back_ref, full)
    picks = [p.astype(F32).astype(BF16) for p in select_rows(ids_ref[...], experts, stride)]
    width = ups_ref.shape[1]
    tile = 512
    total = [jnp.zeros((ups_ref.shape[0], 1), F32) for _ in picks]
    for step in range(width // tile):
        cols = slice(step * tile, (step + 1) * tile)
        ups = ups_ref[:, cols].astype(F32)
        result = None
        for k, pick in enumerate(picks):
            rows = lax.dot_general(pick, full[:, cols], (((0,), (0,)), ((), ())), preferred_element_type=F32)
            part = gates_ref[:, k : k + 1] * rows
            result = part if result is None else result + part
            total[k] = total[k] + jnp.sum(ups * rows, 1, keepdims=True)
        out_ref[:, cols] = result.astype(BF16)
    for k in range(len(picks)):
        dgates_ref[:, k : k + 1] = total[k]


def fill_slots(experts, capacity, stride, back_ref, full):
    if stride != capacity:
        full[...] = jnp.zeros_like(full)
    for e in range(experts):
        full[e * stride : e * stride + capacity, :] = back_ref[e]


def combine_out(ids, gates, upstream, back, experts, capacity):
    rows, width = upstream.shape
    return pl.pallas_call(
        functools.partial(combine_out_kernel, experts, capacity),
        out_shape=(jax.ShapeDtypeStruct((rows, width), BF16), jax.ShapeDtypeStruct(gates.shape, F32)),
        in_specs=[VMEM] * 4,
        out_specs=(VMEM, VMEM),
        scratch_shapes=[pltpu.VMEM((experts * round_up(capacity, 8), width), BF16)],
        cost_estimate=cost(0, nbytes(upstream, upstream, back) * 3),
        name="combine_out",
    )(ids, gates, upstream, back)


def combine_grad_kernel(experts, capacity, ids_ref, back_ref, out_ref, full):
    stride = round_up(capacity, 8)
    fill_slots(experts, capacity, stride, back_ref, full)
    picks = select_rows(ids_ref[...], experts, stride)
    pick = sum(p.astype(F32) for p in picks).astype(BF16)
    width = out_ref.shape[1]
    tile = 512
    for step in range(width // tile):
        cols = slice(step * tile, (step + 1) * tile)
        rows = lax.dot_general(pick, full[:, cols], (((0,), (0,)), ((), ())), preferred_element_type=F32)
        out_ref[:, cols] = rows.astype(BF16)


def combine_grad(ids, back, rows, experts, capacity):
    width = back.shape[2]
    return pl.pallas_call(
        functools.partial(combine_grad_kernel, experts, capacity),
        out_shape=jax.ShapeDtypeStruct((rows, width), BF16),
        in_specs=[VMEM] * 2,
        out_specs=VMEM,
        scratch_shapes=[pltpu.VMEM((experts * round_up(capacity, 8), width), BF16)],
        cost_estimate=cost(0, nbytes(back) * 4),
        name="combine_grad",
    )(ids, back)


def load_pieces(refs, buffers, sems):
    copies = [pltpu.make_async_copy(r, b, sems.at[p]) for p, (r, b) in enumerate(zip(refs, buffers))]
    for copy in copies:
        copy.start()
    return copies


def project(inputs_ref, offsets, pieces, buffers, sems, total_ref):
    copies = load_pieces(pieces, buffers, sems)
    for p, copy in enumerate(copies):
        copy.wait()
        rows = buffers[p].shape[0]
        left = inputs_ref[:, pl.ds(pl.multiple_of(offsets[p], 128), rows)]
        part = jnp.dot(left, buffers[p][...], preferred_element_type=F32)
        if p == 0:
            total_ref[...] = part
        else:
            total_ref[...] += part


def gate_kernel(n, offsets, inputs_ref, *refs):
    pieces, total_ref = refs[:n], refs[n]
    project(inputs_ref, offsets, pieces, refs[n + 1 : 2 * n + 1], refs[-1], total_ref)


def up_kernel(n, offsets, inputs_ref, gate_ref, *refs):
    pieces, up_ref, hidden_ref = refs[:n], refs[n], refs[n + 1]
    project(inputs_ref, offsets, pieces, refs[n + 2 : 2 * n + 2], refs[-1], up_ref)
    gate = gate_ref[...]
    hidden_ref[...] = (gate * jax.nn.sigmoid(gate) * up_ref[...]).astype(BF16)


def piece_scratch(pieces):
    return [pltpu.VMEM(p.shape, p.dtype) for p in pieces] + [pltpu.SemaphoreType.DMA((len(pieces),))]


def gate_projection(inputs, pieces, offsets):
    n = len(pieces)
    total = jax.ShapeDtypeStruct((inputs.shape[0], pieces[0].shape[1]), F32)
    return pl.pallas_call(
        functools.partial(gate_kernel, n),
        out_shape=total,
        in_specs=[SMEM, VMEM] + [ANY] * n,
        out_specs=VMEM,
        scratch_shapes=piece_scratch(pieces),
        cost_estimate=cost(2 * inputs.size * total.shape[1], nbytes(inputs, *pieces)),
        name="gate_projection",
    )(offsets, inputs, *pieces)


def up_projection(inputs, gate_pre, pieces, offsets):
    n = len(pieces)
    return pl.pallas_call(
        functools.partial(up_kernel, n),
        out_shape=(jax.ShapeDtypeStruct(gate_pre.shape, F32), jax.ShapeDtypeStruct(gate_pre.shape, BF16)),
        in_specs=[SMEM, VMEM, VMEM] + [ANY] * n,
        out_specs=(VMEM, VMEM),
        scratch_shapes=piece_scratch(pieces),
        cost_estimate=cost(2 * inputs.size * gate_pre.shape[1], nbytes(inputs, *pieces)),
        name="up_projection",
    )(offsets, inputs, gate_pre, *pieces)


def load_down(n, row_at, col_at, pieces, full, sems):
    copies = []
    for p in range(n):
        rows, cols = pieces[p].shape
        place = full.at[
            pl.ds(pl.multiple_of(row_at[p], 16), rows), pl.ds(pl.multiple_of(col_at[p], 128), cols)
        ]
        copies.append(pltpu.make_async_copy(pieces[p], place, sems.at[p]))
    for copy in copies:
        copy.start()
    for copy in copies:
        copy.wait()


def down_kernel(n, row_at, col_at, hidden_ref, *refs):
    pieces, out_ref, full, sems = refs[:n], refs[n], refs[n + 1], refs[n + 2]
    load_down(n, row_at, col_at, pieces, full, sems)
    out_ref[...] = jnp.dot(hidden_ref[...], full[...], preferred_element_type=F32).astype(BF16)


def down_projection(hidden, pieces, row_at, col_at):
    n = len(pieces)
    slots, width = hidden.shape[0], pieces[0].shape[1]
    return pl.pallas_call(
        functools.partial(down_kernel, n),
        out_shape=jax.ShapeDtypeStruct((slots, width), BF16),
        in_specs=[SMEM, SMEM, VMEM] + [ANY] * n,
        out_specs=VMEM,
        scratch_shapes=[
            pltpu.VMEM((hidden.shape[1], width), BF16),
            pltpu.SemaphoreType.DMA((n,)),
        ],
        cost_estimate=cost(2 * hidden.size * width, nbytes(hidden, *pieces)),
        name="down_projection",
    )(row_at, col_at, hidden, *pieces)


def hidden_grad_kernel(n, row_at, col_at, grads_ref, gate_ref, up_ref, *refs):
    pieces, gate_grad_ref, up_grad_ref, full, sems = refs[:n], refs[n], refs[n + 1], refs[n + 2], refs[n + 3]
    load_down(n, row_at, col_at, pieces, full, sems)
    hidden_grad = lax.dot_general(
        grads_ref[...], full[...], (((1,), (1,)), ((), ())), preferred_element_type=F32
    )
    gate = gate_ref[...]
    squash = jax.nn.sigmoid(gate)
    active = gate * squash
    gate_grad_ref[...] = (hidden_grad * up_ref[...] * (squash + active * (1.0 - squash))).astype(BF16)
    up_grad_ref[...] = (hidden_grad * active).astype(BF16)


def hidden_gradients(grads, gate_pre, up_pre, pieces, row_at, col_at):
    n = len(pieces)
    shape = jax.ShapeDtypeStruct(gate_pre.shape, BF16)
    return pl.pallas_call(
        functools.partial(hidden_grad_kernel, n),
        out_shape=(shape, shape),
        in_specs=[SMEM, SMEM, VMEM, VMEM, VMEM] + [ANY] * n,
        out_specs=(VMEM, VMEM),
        scratch_shapes=[
            pltpu.VMEM((gate_pre.shape[1], grads.shape[1]), BF16),
            pltpu.SemaphoreType.DMA((n,)),
        ],
        cost_estimate=cost(2 * grads.size * gate_pre.shape[1], nbytes(grads, *pieces)),
        name="hidden_gradients",
    )(row_at, col_at, grads, gate_pre, up_pre, *pieces)


def slot_grad_kernel(n, offsets, gate_grad_ref, up_grad_ref, *refs):
    pieces, out_ref = refs[: 2 * n], refs[2 * n]
    buffers, sems = refs[2 * n + 1 : 4 * n + 1], refs[-1]
    copies = load_pieces(pieces, buffers, sems)
    for p in range(n):
        copies[p].wait()
        copies[n + p].wait()
        rows = buffers[p].shape[0]
        part = lax.dot_general(
            gate_grad_ref[...], buffers[p][...], (((1,), (1,)), ((), ())), preferred_element_type=F32
        ) + lax.dot_general(
            up_grad_ref[...], buffers[n + p][...], (((1,), (1,)), ((), ())), preferred_element_type=F32
        )
        out_ref[:, pl.ds(pl.multiple_of(offsets[p], 128), rows)] = part.astype(BF16)


def slot_gradients(gate_grad, up_grad, gate_pieces, up_pieces, offsets, width):
    n = len(gate_pieces)
    pieces = list(gate_pieces) + list(up_pieces)
    return pl.pallas_call(
        functools.partial(slot_grad_kernel, n),
        out_shape=jax.ShapeDtypeStruct((gate_grad.shape[0], width), BF16),
        in_specs=[SMEM, VMEM, VMEM] + [ANY] * (2 * n),
        out_specs=VMEM,
        scratch_shapes=piece_scratch(pieces),
        cost_estimate=cost(4 * gate_grad.size * width, nbytes(*pieces)),
        name="slot_gradients",
    )(offsets, gate_grad, up_grad, *pieces)


def from_ahead(value, axis, step):
    size = lax.axis_size(axis)
    return lax.ppermute(value, axis, [((j + step) % size, j) for j in range(size)])


def relayed(shard, cut_axis):
    n_replica, n_group = lax.axis_size("dp"), lax.axis_size("groups")
    replica, group = lax.axis_index("dp"), lax.axis_index("groups")
    part = shard.shape[cut_axis] // n_group
    mine = lax.dynamic_slice_in_dim(shard, group * part, part, cut_axis)
    pieces = []
    for step in range(1, n_replica):
        source = (replica + step) % n_replica
        piece = from_ahead(mine, "dp", step)
        pieces.append((piece, source, group))
        for hop in range(1, n_group):
            pieces.append((from_ahead(piece, "groups", hop), source, (group + hop) % n_group))
    return pieces


def outer(first_op, second_op):
    product = lax.dot_general(first_op, second_op, (((0,), (0,)), ((), ())), preferred_element_type=F32)
    return product.astype(BF16)


def replica_sum(parts):
    total = parts[0].astype(F32)
    for part in parts[1:]:
        total = total + lax.optimization_barrier(part).astype(F32)
    return total.astype(BF16)


def exchange(value):
    return lax.all_to_all(value, ("expert", "pair"), split_axis=0, concat_axis=0, tiled=True)


def per_device(tokens, expert_ids, gate_weights, upstream, w_gate, w_up, w_down):
    tok_rows, width = tokens.shape
    chosen = expert_ids.shape[1]
    experts = lax.axis_size("expert") * lax.axis_size("pair")
    n_replica = lax.axis_size("dp")
    replica = lax.axis_index("dp")
    capacity = max(2, tok_rows * chosen * 9 // (experts * 8))
    slots = experts * capacity
    w_gate, w_up, w_down = w_gate[0], w_up[0], w_down[0]
    depth, hidden_width = w_gate.shape
    part = depth // lax.axis_size("groups")

    gate_parts = relayed(w_gate, 0)
    up_parts = relayed(w_up, 0)
    down_parts = relayed(w_down, 1)
    offsets = jnp.stack([replica * depth] + [r * depth + g * part for _, r, g in gate_parts])
    row_at = jnp.stack([replica * w_down.shape[0]] + [r * w_down.shape[0] for _, r, _ in down_parts])
    col_at = jnp.stack(
        [jnp.zeros_like(replica)] + [g * (width // lax.axis_size("groups")) for _, _, g in down_parts]
    )
    gate_pieces = [w_gate] + [p for p, _, _ in gate_parts]
    up_pieces = [w_up] + [p for p, _, _ in up_parts]
    down_pieces = [w_down] + [p for p, _, _ in down_parts]

    ids = expert_ids.T
    send_rows, send_grads = dispatch(ids, gate_weights.T, tokens, upstream, experts, capacity)
    rows = exchange(send_rows).reshape(slots, width)
    grads = exchange(send_grads).reshape(slots, width)

    gate_pre = gate_projection(rows, gate_pieces, offsets)
    up_pre, hidden = up_projection(rows, gate_pre, up_pieces, offsets)
    output = down_projection(hidden, down_pieces, row_at, col_at)
    gate_grad, up_grad = hidden_gradients(grads, gate_pre, up_pre, down_pieces, row_at, col_at)
    slot_grad = slot_gradients(gate_grad, up_grad, gate_pieces, up_pieces, offsets, width)
    back_out = exchange(output.reshape(experts, capacity, width))
    back_grad = exchange(slot_grad.reshape(experts, capacity, width))

    shard = w_down.shape[0]
    window = max(i * shard % 128 + shard for i in range(n_replica))
    window = min(hidden_width, round_up(window, 128))

    def window_at(index):
        return jnp.minimum(index * shard // 128 * 128, hidden_width - window)

    def row_block(index):
        return lax.dynamic_slice_in_dim(rows, index * depth, depth, 1)

    def hidden_block(index):
        return lax.dynamic_slice_in_dim(hidden, window_at(index), window, 1)

    mine_rows, mine_hidden = row_block(replica), hidden_block(replica)
    gate_sum, up_sum, down_sum = [outer(mine_rows, gate_grad)], [outer(mine_rows, up_grad)], [outer(mine_hidden, grads)]
    for step in range(1, n_replica):
        target = (replica - step) % n_replica
        got_rows = from_ahead(row_block(target), "dp", step)
        got_grads = from_ahead(grads, "dp", step)
        got_hidden = from_ahead(hidden_block(target), "dp", step)
        got_gate = from_ahead(gate_grad, "dp", step)
        got_up = from_ahead(up_grad, "dp", step)
        down_sum.append(outer(got_hidden, got_grads))
        gate_sum.append(outer(got_rows, got_gate))
        up_sum.append(outer(got_rows, got_up))
    grad_gate = replica_sum(gate_sum)[None]
    grad_up = replica_sum(up_sum)[None]
    grad_down = lax.dynamic_slice_in_dim(
        replica_sum(down_sum), replica * shard - window_at(replica), shard, 0
    )[None]

    result, d_gates = combine_out(ids, gate_weights, upstream, back_out, experts, capacity)
    d_tokens = combine_grad(ids, back_grad, tok_rows, experts, capacity)
    return (result, d_tokens, d_gates, grad_gate, grad_up, grad_down)


def solution(mesh):
    return jax.shard_map(
        per_device,
        mesh=mesh,
        in_specs=(
            P(("groups", "expert", "dp", "pair"), None),
            P(("groups", "expert", "dp", "pair"), None),
            P(("groups", "expert", "dp", "pair"), None),
            P(("groups", "expert", "dp", "pair"), None),
            P(("expert", "pair"), "dp", None),
            P(("expert", "pair"), "dp", None),
            P(("expert", "pair"), "dp", None),
        ),
        out_specs=(
            P(("groups", "expert", "dp", "pair"), None),
            P(("groups", "expert", "dp", "pair"), None),
            P(("groups", "expert", "dp", "pair"), None),
            P(("groups", "expert", "pair"), "dp", None),
            P(("groups", "expert", "pair"), "dp", None),
            P(("groups", "expert", "pair"), "dp", None),
        ),
        check_vma=False,
    )
```
